256 devices in a mesh: chan: 64 (over y, z_hi, x), hour: 4 (over z_lo, core).
Axes of the slice: x: 4, y: 4, z: 8 (z_hi: 4, z_lo: 2; z = z_hi * 2 + z_lo), core: 2. Of those that a mesh axis runs over, the one named last changes fastest.
Arguments:
- spectra: bfloat16 [2, 64, 800, 8192], P(None, 'hour', None, 'chan'), may hold values from -6 to 6
- quality: int32 [64, 8192], P('hour', 'chan'), may hold values 0 or 1
- sources: int32 [32], replicated, may hold values from 0 to 8191
Outputs:
- correlation: bfloat16 [32, 512, 8192], P('hour', None, 'chan')
The draws below stay inside these ranges and needn't reach their ends.
Inputs may be any that keep to these rules, and one draw needn't show every extreme that they name: `sources`: indices may repeat.
All inputs are finite; a program needn't handle non-finite values. No bound on the sum of `quality` on one device may be relied on, other than what follows from the above.
Results may differ from the reference program's by a relative error of at most 0.01.
Values may be sent and summed in bfloat16 or wider, within the bound.
A program may use at most 128 MiB of HBM per device.

```python
import math
import jax
import jax.numpy as jnp
from jax import lax

C_DEV = 128
W_DEV = 16
F_BINS = 800
LAGS = 512
S_SRC = 32
CHANNELS = 8192
WINDOWS = 64
N_HOUR = 4


def with_ends(result, rng, low, high):
    dims = result.shape
    index_at = [jax.random.randint(jax.random.fold_in(rng, axis), (), 0, dims[axis]) for axis in range(len(dims))]
    result = result.at[tuple(index_at)].set(low)
    longest = dims.index(max(dims))
    index_at[longest] = (index_at[longest] + 1) % dims[longest]
    return result.at[tuple(index_at)].set(high)


def level_of(rng, shape, split, low, top_value):
    def one(position, shards_of):
        steps = jax.random.uniform(jax.random.fold_in(jax.random.fold_in(rng, 6), position), (shards_of,), jnp.float32, low / len(split), top_value / len(split))
        return jnp.repeat(jnp.exp(steps), shape[position] // shards_of).reshape((-1,) + (1,) * (len(shape) - position - 1))

    loudness = one(*split[0])
    for cut in split[1:]:
        loudness = loudness * one(*cut)
    return loudness


def centred(stream_key, extent, deviation, most, split=(), kind=jnp.bfloat16):
    result = deviation * jax.random.normal(stream_key, extent, jnp.float32)
    if split:
        result = result * level_of(stream_key, extent, split, -0.22, 0.18)
    return jnp.clip(result, -most, most).astype(kind)


def setup_inputs(seed: int = 0) -> dict:
    streams_of = jax.random.split(jax.random.key(seed), 4)
    spectra = centred(streams_of[0], (2, WINDOWS, F_BINS, CHANNELS), 1.0, 6.0, ((1, 4), (3, 64)))
    quality = with_ends((jax.random.randint(streams_of[1], (WINDOWS, CHANNELS), 0, 4) < 3).astype(jnp.int32), jax.random.fold_in(streams_of[1], 1), 0, 1)
    sources = with_ends(jax.random.randint(streams_of[2], (S_SRC,), 0, CHANNELS), jax.random.fold_in(streams_of[2], 1), 0, CHANNELS - 1).astype(jnp.int32)
    return dict(spectra=spectra, quality=quality, sources=sources)


def whiten(record, usable):
    as_float = record.astype(jnp.float32)
    power = lax.optimization_barrier(jnp.mean(as_float[0] * as_float[0] + as_float[1] * as_float[1], axis=1))
    scale = lax.rsqrt(power + 1e-06) * usable.astype(jnp.float32)
    return (as_float * scale[None, :, None, :]).astype(jnp.bfloat16)

def lag_table(freq_count, lag_count):
    bin_number = jnp.arange(freq_count, dtype=jnp.float32) + 1.0
    lag_offset = jnp.arange(lag_count, dtype=jnp.float32) - float(lag_count // 2)
    phase = math.pi * bin_number[:, None] * lag_offset[None, :] / freq_count
    return (jnp.stack([jnp.cos(phase), -jnp.sin(phase)]) / freq_count).astype(jnp.bfloat16)

def cross_spectrum(source_spec, receivers):
    left_real = source_spec.astype(jnp.float32)
    right_real = receivers.astype(jnp.float32)
    real_part = jnp.einsum('kwfs,kwfc->fsc', left_real, right_real)
    left_pair = jnp.stack([left_real[0], -left_real[1]])
    right_pair = jnp.stack([right_real[1], right_real[0]])
    imag_part = jnp.einsum('kwfs,kwfc->fsc', left_pair, right_pair)
    return jnp.stack([real_part, imag_part]).astype(jnp.bfloat16)

def reference(spectra, quality, sources):
    source_spec = whiten(spectra[:, :, :, sources], quality[:, sources])
    table = lag_table(F_BINS, LAGS).astype(jnp.float32)

    def one_block(block_id):
        first = (block_id * C_DEV).astype(jnp.int32)
        raw = lax.dynamic_slice_in_dim(spectra, first, C_DEV, 3)
        usable = lax.dynamic_slice_in_dim(quality, first, C_DEV, 1)
        receivers = whiten(raw, usable)
        total = jnp.zeros((S_SRC, LAGS, C_DEV), jnp.float32)
        for hour_id in range(N_HOUR):
            low = hour_id * W_DEV
            partial_value = cross_spectrum(source_spec[:, low:low + W_DEV], receivers[:, low:low + W_DEV])
            total = total + jnp.einsum('kfsc,kfl->slc', partial_value.astype(jnp.float32), table)
        return total.astype(jnp.bfloat16)
    blocks = lax.map(one_block, jnp.arange(CHANNELS // C_DEV, dtype=jnp.int32))
    return blocks.transpose(1, 2, 0, 3).reshape(S_SRC, LAGS, CHANNELS)
```

```python
import jax
import jax.numpy as jnp
import numpy as np
from jax import lax
from jax.experimental import pallas as pl
from jax.experimental.pallas import tpu as pltpu
from jax.sharding import PartitionSpec as P

LAGS = 512
F32 = jnp.float32
BF16 = jnp.bfloat16
BLOCKS = 100
ROWS = 112
QUARTER = 28
PIECE = 7
DEPTH = 1664


def lag_table(freq_count):
    bin_number = np.arange(freq_count, dtype=np.float32) + np.float32(1.0)
    lag_offset = np.arange(LAGS, dtype=np.float32) - np.float32(LAGS // 2)
    phase = np.float32(np.pi) * bin_number[:, None] * lag_offset[None, :] / np.float32(freq_count)
    table = np.concatenate([np.cos(phase), -np.sin(phase)], 0) / np.float32(freq_count)
    table = np.concatenate([table, np.zeros((DEPTH - 2 * freq_count, LAGS), np.float32)], 0)
    return np.ascontiguousarray(table.T).astype(BF16)


def kernel(
    sources, spectra, quality, table_hbm, out_hbm,
    w, table, first, got1, sum1, got2, sum2, got3, sum3, got4, spec, part,
    to_core, from_core, to_chip, from_chip, kept, out,
    load_sem, table_sem, out_sem, send_sem, recv_sem, core_send, core_recv, chip_send, chip_recv,
):
    chan, hour = lax.axis_index("chan"), lax.axis_index("hour")
    y, zh, x = chan // 16, (chan // 4) % 4, chan % 4
    zl, core = hour // 2, hour % 2

    def at(ny, nzh, nx):
        return (ny * 16 + nzh * 4 + nx, hour)

    def along(axis, d):
        return at(y, zh, (x + d) % 4) if axis == 0 else at((y + d) % 4, zh, x)

    pair_a = at(y, zh + 1 - 2 * (zh % 2), x)
    pair_b = at(y, 3 - zh, x)
    core_peer = (chan, zl * 2 + 1 - core)
    chip_peer = (chan, (1 - zl) * 2 + core)

    loads = [
        pltpu.make_async_copy(
            spectra.at[kw // 16, kw % 16], w.at[:, pl.ds(kw * 8, 8), :], load_sem.at[kw]
        )
        for kw in range(32)
    ]
    for copy in loads:
        copy.start()
    load_table = pltpu.make_async_copy(table_hbm, table, table_sem)
    load_table.start()

    barrier = pltpu.get_barrier_semaphore()
    peers = [along(axis, d) for axis in range(2) for d in range(1, 4)]
    peers += [pair_a, pair_b, core_peer, chip_peer]
    for peer in peers:
        pl.semaphore_signal(barrier, inc=1, device_id=peer, device_id_type=pl.DeviceIdType.MESH)

    row = lax.broadcasted_iota(jnp.int32, (32, 128), 0)
    lane = lax.broadcasted_iota(jnp.int32, (32, 128), 1)
    wanted = jnp.zeros((32, 128), jnp.int32)
    for r in range(32):
        q, i = r // 8, r % 8
        chip = (1 - zl) if q < 2 else zl
        index = (chip * 2 + i // 4) * 8 + (q % 2) * 4 + i % 4
        wanted = jnp.where(row == r, sources[index], wanted)
    onehot = jnp.where(lane + chan * 128 == wanted, 1.0, 0.0).astype(BF16)
    usable = quality[...].astype(F32)
    usable_rows = jnp.broadcast_to(usable[:, None, :], (16, 8, 128)).reshape(128, 128)
    nt = (((1,), (1,)), ((), ()))
    usable_src = lax.dot_general(
        onehot, usable_rows.astype(BF16), nt, preferred_element_type=F32
    )
    zero_tile = jnp.zeros((8, 128), BF16)
    for q in range(4):
        for k in range(2):
            for fb in range(BLOCKS, ROWS):
                first[q, k, fb] = zero_tile
    part[:, pl.ds(1600, DEPTH - 1600), :] = jnp.zeros((4, DEPTH - 1600, 256), BF16)

    def pick(q0, q1):
        hot = onehot[q0 * 8:q1 * 8]
        use = usable_src[q0 * 8:q1 * 8]

        def step(fb, _):
            got = lax.dot_general(hot, w[fb], nt, preferred_element_type=F32)
            for q in range(q0, q1):
                rows = slice((q - q0) * 8, (q - q0 + 1) * 8)
                for k in range(2):
                    value = got[rows, k * 128:(k + 1) * 128] * use[rows]
                    first[q, k, fb] = value.astype(BF16)
            return 0

        lax.fori_loop(0, BLOCKS, step, 0, unroll=5)

    def send(src, dst, q, phase, k, d, peer):
        copy = pltpu.make_async_remote_copy(
            src_ref=src, dst_ref=dst,
            send_sem=send_sem.at[q, phase, k, d], recv_sem=recv_sem.at[q, phase, k, d],
            device_id=peer, device_id_type=pl.DeviceIdType.MESH,
        )
        copy.start()
        return copy

    sent = {}
    mine = [(x, y), (y, x)]

    def p1(q):
        for k in range(2):
            for d in range(1, 4):
                to = (mine[k][0] + d) % 4
                sent[q, 1, k, d] = send(
                    first.at[q, k, pl.ds(to * QUARTER, QUARTER)], got1.at[q, k, d - 1],
                    q, 0, k, d - 1, along(k, d),
                )

    def p2(q):
        for k in range(2):
            for d in range(1, 4):
                sent[q, 1, k, d].wait_recv()
            total = first[q, k, pl.ds(mine[k][0] * QUARTER, QUARTER)]
            for d in range(3):
                total = total + got1[q, k, d]
            sum1[q, k] = total
            for d in range(1, 4):
                to = (mine[k][1] + d) % 4
                sent[q, 2, k, d] = send(
                    sum1.at[q, k, pl.ds(to * PIECE, PIECE)], got2.at[q, k, d - 1],
                    q, 1, k, d - 1, along(1 - k, d),
                )

    def p3(q):
        for k in range(2):
            for d in range(1, 4):
                sent[q, 2, k, d].wait_recv()
            total = sum1[q, k, pl.ds(mine[k][1] * PIECE, PIECE)]
            for d in range(3):
                total = total + got2[q, k, d]
            sum2[q, k] = total
            sent[q, 3, k, 1] = send(
                sum2.at[q, k], got3.at[q, k], q, 2, k, 0, (pair_a, pair_b)[k]
            )

    def p4(q):
        for k in range(2):
            sent[q, 3, k, 1].wait_recv()
            sum3[q, k] = sum2[q, k] + got3[q, k]
            sent[q, 4, k, 1] = send(
                sum3.at[q, k], got4.at[q, k], q, 3, k, 0, (pair_b, pair_a)[k]
            )

    def p5(q):
        for k in range(2):
            sent[q, 4, k, 1].wait_recv()
            here = spec.at[q, k, pl.ds(mine[k][0] * QUARTER + mine[k][1] * PIECE, PIECE)]
            here[...] = sum3[q, k] + got4[q, k]
            for d in range(1, 4):
                sent[q, 5, k, d] = send(here, here, q, 4, k, d - 1, along(1 - k, d))

    def p6(q):
        for k in range(2):
            for d in range(1, 4):
                sent[q, 5, k, d].wait_recv()
            here = spec.at[q, k, pl.ds(mine[k][0] * QUARTER, QUARTER)]
            for d in range(1, 4):
                sent[q, 6, k, d] = send(here, here, q, 5, k, d - 1, along(k, d))

    def done(q):
        for k in range(2):
            for d in range(1, 4):
                sent[q, 6, k, d].wait_recv()

    def measure_power():
        def step(fb, total):
            value = w[fb].astype(F32)
            return total + value * value

        total = lax.fori_loop(0, BLOCKS, step, jnp.zeros((256, 128), F32), unroll=5)
        total = jnp.sum(total.reshape(32, 8, 128), axis=1)
        power = (total[:16] + total[16:]) / (BLOCKS * 8)
        scale = lax.rsqrt(power + 1e-06) * usable
        rows = jnp.broadcast_to(scale[:, None, :], (16, 8, 128)).reshape(128, 128)
        return jnp.concatenate([rows, rows], 0)

    def whiten(scale):
        def step(fb, _):
            w[fb] = (w[fb].astype(F32) * scale).astype(BF16)
            return 0

        lax.fori_loop(0, BLOCKS, step, 0, unroll=5)

    diagonal = (
        lax.broadcasted_iota(jnp.int32, (8, 128), 0)
        == lax.broadcasted_iota(jnp.int32, (8, 128), 1) % 8
    )
    same_window = jnp.where(
        lax.broadcasted_iota(jnp.int32, (128, 128), 0) // 8
        == lax.broadcasted_iota(jnp.int32, (128, 128), 1) // 8, 1.0, 0.0
    )

    def cross(q):
        def power_step(fb, total):
            real, imag = spec[q, 0, fb].astype(F32), spec[q, 1, fb].astype(F32)
            return total + real * real + imag * imag

        total = lax.fori_loop(0, BLOCKS, power_step, jnp.zeros((8, 128), F32), unroll=10)
        power = jnp.dot(
            total, same_window, precision=lax.Precision.HIGHEST, preferred_element_type=F32
        ) / (BLOCKS * 8)
        scale = lax.rsqrt(power + 1e-06)

        def step(pair, _):
            outs = []
            for d in range(2):
                fb = pair * 2 + d
                real = spec[q, 0, fb].astype(F32) * scale
                imag = spec[q, 1, fb].astype(F32) * scale
                upper, lower = [], []
                for s in range(8):
                    a = jnp.where(diagonal, jnp.broadcast_to(real[s:s + 1], (8, 128)), 0.0)
                    b = jnp.where(diagonal, jnp.broadcast_to(imag[s:s + 1], (8, 128)), 0.0)
                    upper.append(jnp.concatenate([a, b], 1))
                    lower.append(jnp.concatenate([-b, a], 1))
                left = jnp.concatenate(upper + lower, 0).astype(BF16)
                outs.append(jnp.dot(left, w[fb], preferred_element_type=F32).reshape(2, 8, 8, 128))
            for j in range(2):
                start = pl.multiple_of(j * 800 + pair * 16, 16)
                for s in range(8):
                    value = jnp.concatenate([outs[0][j, s], outs[1][j, s]], 0).astype(BF16)
                    part[s // 2, pl.ds(start, 16), pl.ds((s % 2) * 128, 128)] = value
            return 0

        lax.fori_loop(0, BLOCKS // 2, step, 0, unroll=5)

    def lags(pair):
        value = jnp.dot(table[...], part[pair], preferred_element_type=F32)
        return value[:, :128], value[:, 128:]

    moved = {}

    def stack(q):
        for i in range(2):
            both = lags((1 - core) * 2 + i)
            for s in range(2):
                to_core[q, i, s] = both[s].astype(BF16)
            copy = pltpu.make_async_remote_copy(
                src_ref=to_core.at[q, i], dst_ref=from_core.at[q, i],
                send_sem=core_send.at[q, i], recv_sem=core_recv.at[q, i],
                device_id=core_peer, device_id_type=pl.DeviceIdType.MESH,
            )
            copy.start()
            moved[q, i] = copy
        for i in range(2):
            both = lags(core * 2 + i)
            if q < 2:
                moved[q, i].wait_recv()
                for s in range(2):
                    to_chip[q, i, s] = (both[s] + from_core[q, i, s].astype(F32)).astype(BF16)
                copy = pltpu.make_async_remote_copy(
                    src_ref=to_chip.at[q, i], dst_ref=from_chip.at[q, i],
                    send_sem=chip_send.at[q, i], recv_sem=chip_recv.at[q, i],
                    device_id=chip_peer, device_id_type=pl.DeviceIdType.MESH,
                )
                copy.start()
                moved["chip", q, i] = copy
            else:
                for s in range(2):
                    kept[q - 2, i, s] = both[s]

    stores = []

    def finish(q, i):
        moved[q + 2, i].wait_recv()
        moved["chip", q, i].wait_recv()
        for s in range(2):
            value = kept[q, i, s] + from_core[q + 2, i, s].astype(F32)
            out[q, i, s] = (value + from_chip[q, i, s].astype(F32)).astype(BF16)
        copy = pltpu.make_async_copy(
            out.at[q, i], out_hbm.at[pl.ds(q * 4 + i * 2, 2)], out_sem.at[q, i]
        )
        copy.start()
        stores.append(copy)

    for copy in loads:
        copy.wait()
    pick(0, 1)
    pl.semaphore_wait(barrier, len(peers))
    p1(0)
    pick(1, 4)
    p2(0)
    p1(1)
    scale = measure_power()
    p3(0)
    whiten(scale)
    p4(0)
    p2(1)
    p1(2)
    p5(0)
    p3(1)
    p6(0)
    p4(1)
    p2(2)
    p1(3)
    done(0)
    p5(1)
    p3(2)
    p2(3)
    cross(0)
    p6(1)
    p4(2)
    p3(3)
    load_table.wait()
    stack(0)
    done(1)
    p5(2)
    p4(3)
    cross(1)
    p6(2)
    p5(3)
    stack(1)
    done(2)
    p6(3)
    cross(2)
    stack(2)
    done(3)
    cross(3)
    stack(3)
    for q in range(2):
        for i in range(2):
            finish(q, i)
    for copy in list(sent.values()) + list(moved.values()):
        copy.wait_send()
    for copy in stores:
        copy.wait()


def body(spectra, quality, sources):
    windows, freq_count, channels = spectra.shape[1:]
    any_space = pl.BlockSpec(memory_space=pl.ANY)
    dma = pltpu.SemaphoreType.DMA
    return pl.pallas_call(
        kernel,
        out_shape=jax.ShapeDtypeStruct((8, LAGS, channels), BF16),
        in_specs=[
            pl.BlockSpec(memory_space=pltpu.SMEM),
            any_space,
            pl.BlockSpec(memory_space=pltpu.VMEM),
            any_space,
        ],
        out_specs=any_space,
        scratch_shapes=[
            pltpu.VMEM((BLOCKS, 256, 128), BF16),
            pltpu.VMEM((LAGS, DEPTH), BF16),
            pltpu.VMEM((4, 2, ROWS, 8, 128), BF16),
            pltpu.VMEM((4, 2, 3, QUARTER, 8, 128), BF16),
            pltpu.VMEM((4, 2, QUARTER, 8, 128), BF16),
            pltpu.VMEM((4, 2, 3, PIECE, 8, 128), BF16),
            pltpu.VMEM((4, 2, PIECE, 8, 128), BF16),
            pltpu.VMEM((4, 2, PIECE, 8, 128), BF16),
            pltpu.VMEM((4, 2, PIECE, 8, 128), BF16),
            pltpu.VMEM((4, 2, PIECE, 8, 128), BF16),
            pltpu.VMEM((4, 2, ROWS, 8, 128), BF16),
            pltpu.VMEM((4, DEPTH, 256), BF16),
            pltpu.VMEM((4, 2, 2, LAGS, 128), BF16),
            pltpu.VMEM((4, 2, 2, LAGS, 128), BF16),
            pltpu.VMEM((2, 2, 2, LAGS, 128), BF16),
            pltpu.VMEM((2, 2, 2, LAGS, 128), BF16),
            pltpu.VMEM((2, 2, 2, LAGS, 128), F32),
            pltpu.VMEM((2, 2, 2, LAGS, 128), BF16),
            dma((32,)),
            dma,
            dma((2, 2)),
            dma((4, 6, 2, 3)),
            dma((4, 6, 2, 3)),
            dma((4, 2)),
            dma((4, 2)),
            dma((2, 2)),
            dma((2, 2)),
        ],
        compiler_params=pltpu.CompilerParams(
            collective_id=0, has_side_effects=True, vmem_limit_bytes=60 * 1024 * 1024
        ),
    )(
        sources,
        spectra.reshape(2, windows, BLOCKS, 8, channels),
        quality,
        jnp.asarray(lag_table(freq_count)),
    )


def solution(mesh):
    placed = (P(None, "hour", None, "chan"), P("hour", "chan"), P())
    return jax.shard_map(
        body, mesh=mesh, in_specs=placed, out_specs=P("hour", None, "chan"), check_vma=False
    )
```

```python
import jax
import jax.numpy as jnp
import numpy as np
from jax import lax
from jax.experimental import pallas as pl
from jax.experimental.pallas import tpu as pltpu
from jax.sharding import PartitionSpec as P

LAGS = 512
F32 = jnp.float32
BF16 = jnp.bfloat16
BLOCKS = 100
ROWS = 112
QUARTER = 28
PIECE = 7
DEPTH = 1664


def lag_table(freq_count):
    bin_number = np.arange(freq_count, dtype=np.float32) + np.float32(1.0)
    lag_offset = np.arange(LAGS, dtype=np.float32) - np.float32(LAGS // 2)
    phase = np.float32(np.pi) * bin_number[:, None] * lag_offset[None, :] / np.float32(freq_count)
    table = np.concatenate([np.cos(phase), -np.sin(phase)], 0) / np.float32(freq_count)
    table = np.concatenate([table, np.zeros((DEPTH - 2 * freq_count, LAGS), np.float32)], 0)
    return np.ascontiguousarray(table.T).astype(BF16)


def kernel(
    sources, spectra, quality, table_hbm, out_hbm,
    w, table, first, got1, sum1, got2, sum2, got3, spec, part,
    to_core, from_core, to_chip, from_chip, kept, out,
    load_sem, table_sem, out_sem, send_sem, recv_sem, core_send, core_recv, chip_send, chip_recv,
):
    chan, hour = lax.axis_index("chan"), lax.axis_index("hour")
    y, zh, x = chan // 16, (chan // 4) % 4, chan % 4
    zl, core = hour // 2, hour % 2

    def at(ny, nzh, nx):
        return (ny * 16 + nzh * 4 + nx, hour)

    quarters = [(r * QUARTER, min(QUARTER, BLOCKS - r * QUARTER)) for r in range(4)]

    def along(axis, d):
        return at(y, zh, (x + d) % 4) if axis == 0 else at((y + d) % 4, zh, x)

    core_peer = (chan, zl * 2 + 1 - core)
    chip_peer = (chan, (1 - zl) * 2 + core)

    loads = [
        [
            pltpu.make_async_copy(
                spectra.at[kw // 16, kw % 16, pl.ds(low, size)],
                w.at[pl.ds(low, size), pl.ds(kw * 8, 8), :], load_sem.at[r, kw],
            )
            for kw in range(32)
        ]
        for r, (low, size) in enumerate(quarters)
    ]
    for group in loads:
        for copy in group:
            copy.start()
    load_table = pltpu.make_async_copy(table_hbm, table, table_sem)
    load_table.start()

    barrier = pltpu.get_barrier_semaphore()
    peers = [along(axis, d) for axis in range(2) for d in range(1, 4)]
    peers += [at(y, (zh + d) % 4, x) for d in range(1, 4)] + [core_peer, chip_peer]
    for peer in peers:
        pl.semaphore_signal(barrier, inc=1, device_id=peer, device_id_type=pl.DeviceIdType.MESH)

    row = lax.broadcasted_iota(jnp.int32, (32, 128), 0)
    lane = lax.broadcasted_iota(jnp.int32, (32, 128), 1)
    wanted = jnp.zeros((32, 128), jnp.int32)
    for r in range(32):
        q, i = r // 8, r % 8
        chip = (1 - zl) if q < 2 else zl
        index = (chip * 2 + i // 4) * 8 + (q % 2) * 4 + i % 4
        wanted = jnp.where(row == r, sources[index], wanted)
    onehot = jnp.where(lane + chan * 128 == wanted, 1.0, 0.0).astype(BF16)
    usable = quality[...].astype(F32)
    usable_rows = jnp.broadcast_to(usable[:, None, :], (16, 8, 128)).reshape(128, 128)
    nt = (((1,), (1,)), ((), ()))
    usable_src = lax.dot_general(
        onehot, usable_rows.astype(BF16), nt, preferred_element_type=F32
    )
    zero_tile = jnp.zeros((8, 128), BF16)
    for q in range(4):
        for k in range(2):
            for fb in range(BLOCKS, ROWS):
                first[q, k, fb] = zero_tile
    part[:, pl.ds(1600, DEPTH - 1600), :] = jnp.zeros((4, DEPTH - 1600, 256), BF16)

    def pick(q0, q1, low, high):
        hot = onehot[q0 * 8:q1 * 8]
        use = usable_src[q0 * 8:q1 * 8]

        def step(fb, _):
            got = lax.dot_general(hot, w[fb], nt, preferred_element_type=F32)
            for q in range(q0, q1):
                rows = slice((q - q0) * 8, (q - q0 + 1) * 8)
                for k in range(2):
                    value = got[rows, k * 128:(k + 1) * 128] * use[rows]
                    first[q, k, fb] = value.astype(BF16)
            return 0

        lax.fori_loop(low, high, step, 0, unroll=4)

    def send(src, dst, q, phase, k, d, peer):
        copy = pltpu.make_async_remote_copy(
            src_ref=src, dst_ref=dst,
            send_sem=send_sem.at[q, phase, k, d], recv_sem=recv_sem.at[q, phase, k, d],
            device_id=peer, device_id_type=pl.DeviceIdType.MESH,
        )
        copy.start()
        return copy

    sent = {}
    mine = [(x, y), (y, x)]

    def p1_copy(q, k, to, slot):
        peer = at(y, zh, to) if k == 0 else at(to, zh, x)
        return pltpu.make_async_remote_copy(
            src_ref=first.at[q, k, pl.ds(to * QUARTER, QUARTER)], dst_ref=got1.at[q, k, slot],
            send_sem=send_sem.at[q, 0, k, slot], recv_sem=recv_sem.at[q, 0, k, slot],
            device_id=peer, device_id_type=pl.DeviceIdType.MESH,
        )

    def p1_quarter(q, r):
        for k in range(2):
            @pl.when(mine[k][0] != r)
            def _():
                p1_copy(q, k, r, (r + 3 - mine[k][0]) % 4).start()

    def p1_expect(q):
        for k in range(2):
            for d in range(1, 4):
                sent[q, 1, k, d] = p1_copy(q, k, (mine[k][0] + d) % 4, d - 1)

    def p1(q):
        p1_expect(q)
        for k in range(2):
            for d in range(1, 4):
                sent[q, 1, k, d].start()

    def p2(q):
        for k in range(2):
            for d in range(1, 4):
                sent[q, 1, k, d].wait_recv()
            total = first[q, k, pl.ds(mine[k][0] * QUARTER, QUARTER)]
            for d in range(3):
                total = total + got1[q, k, d]
            sum1[q, k] = total
            for d in range(1, 4):
                to = (mine[k][1] + d) % 4
                sent[q, 2, k, d] = send(
                    sum1.at[q, k, pl.ds(to * PIECE, PIECE)], got2.at[q, k, d - 1],
                    q, 1, k, d - 1, along(1 - k, d),
                )

    def p3(q):
        for k in range(2):
            for d in range(1, 4):
                sent[q, 2, k, d].wait_recv()
            total = sum1[q, k, pl.ds(mine[k][1] * PIECE, PIECE)]
            for d in range(3):
                total = total + got2[q, k, d]
            sum2[q, k] = total
            for d in (2, 1, 3):
                sent[q, 3, k, d] = send(
                    sum2.at[q, k], got3.at[q, k, d - 1], q, 2, k, d - 1, at(y, (zh + d) % 4, x)
                )

    def p5(q):
        for k in range(2):
            for d in range(1, 4):
                sent[q, 3, k, d].wait_recv()
            total = sum2[q, k]
            for d in range(3):
                total = total + got3[q, k, d]
            here = spec.at[q, k, pl.ds(mine[k][0] * QUARTER + mine[k][1] * PIECE, PIECE)]
            here[...] = total
            for d in range(1, 4):
                sent[q, 5, k, d] = send(here, here, q, 4, k, d - 1, along(1 - k, d))

    def p6(q):
        for k in range(2):
            for d in range(1, 4):
                sent[q, 5, k, d].wait_recv()
            here = spec.at[q, k, pl.ds(mine[k][0] * QUARTER, QUARTER)]
            for d in range(1, 4):
                sent[q, 6, k, d] = send(here, here, q, 5, k, d - 1, along(k, d))

    def done(q):
        for k in range(2):
            for d in range(1, 4):
                sent[q, 6, k, d].wait_recv()

    def measure_power():
        def step(fb, total):
            value = w[fb].astype(F32)
            return total + value * value

        total = lax.fori_loop(0, BLOCKS, step, jnp.zeros((256, 128), F32), unroll=5)
        total = jnp.sum(total.reshape(32, 8, 128), axis=1)
        power = (total[:16] + total[16:]) / (BLOCKS * 8)
        scale = lax.rsqrt(power + 1e-06) * usable
        rows = jnp.broadcast_to(scale[:, None, :], (16, 8, 128)).reshape(128, 128)
        return jnp.concatenate([rows, rows], 0)

    def whiten(scale):
        def step(fb, _):
            w[fb] = (w[fb].astype(F32) * scale).astype(BF16)
            return 0

        lax.fori_loop(0, BLOCKS, step, 0, unroll=5)

    diagonal = (
        lax.broadcasted_iota(jnp.int32, (8, 128), 0)
        == lax.broadcasted_iota(jnp.int32, (8, 128), 1) % 8
    )
    same_window = jnp.where(
        lax.broadcasted_iota(jnp.int32, (128, 128), 0) // 8
        == lax.broadcasted_iota(jnp.int32, (128, 128), 1) // 8, 1.0, 0.0
    )

    def cross(q):
        def power_step(fb, total):
            real, imag = spec[q, 0, fb].astype(F32), spec[q, 1, fb].astype(F32)
            return total + real * real + imag * imag

        total = lax.fori_loop(0, BLOCKS, power_step, jnp.zeros((8, 128), F32), unroll=10)
        power = jnp.dot(
            total, same_window, precision=lax.Precision.HIGHEST, preferred_element_type=F32
        ) / (BLOCKS * 8)
        scale = lax.rsqrt(power + 1e-06)

        def step(pair, _):
            outs = []
            for d in range(2):
                fb = pair * 2 + d
                real = spec[q, 0, fb].astype(F32) * scale
                imag = spec[q, 1, fb].astype(F32) * scale
                upper, lower = [], []
                for s in range(8):
                    a = jnp.where(diagonal, jnp.broadcast_to(real[s:s + 1], (8, 128)), 0.0)
                    b = jnp.where(diagonal, jnp.broadcast_to(imag[s:s + 1], (8, 128)), 0.0)
                    upper.append(jnp.concatenate([a, b], 1))
                    lower.append(jnp.concatenate([-b, a], 1))
                left = jnp.concatenate(upper + lower, 0).astype(BF16)
                outs.append(jnp.dot(left, w[fb], preferred_element_type=F32).reshape(2, 8, 8, 128))
            for j in range(2):
                start = pl.multiple_of(j * 800 + pair * 16, 16)
                for s in range(8):
                    value = jnp.concatenate([outs[0][j, s], outs[1][j, s]], 0).astype(BF16)
                    part[s // 2, pl.ds(start, 16), pl.ds((s % 2) * 128, 128)] = value
            return 0

        lax.fori_loop(0, BLOCKS // 2, step, 0, unroll=5)

    def lags(pair):
        value = jnp.dot(table[...], part[pair], preferred_element_type=F32)
        return value[:, :128], value[:, 128:]

    moved = {}

    def stack(q):
        for i in range(2):
            both = lags((1 - core) * 2 + i)
            for s in range(2):
                to_core[q, i, s] = both[s].astype(BF16)
            copy = pltpu.make_async_remote_copy(
                src_ref=to_core.at[q, i], dst_ref=from_core.at[q, i],
                send_sem=core_send.at[q, i], recv_sem=core_recv.at[q, i],
                device_id=core_peer, device_id_type=pl.DeviceIdType.MESH,
            )
            copy.start()
            moved[q, i] = copy
        for i in range(2):
            both = lags(core * 2 + i)
            if q < 2:
                moved[q, i].wait_recv()
                for s in range(2):
                    to_chip[q, i, s] = (both[s] + from_core[q, i, s].astype(F32)).astype(BF16)
                copy = pltpu.make_async_remote_copy(
                    src_ref=to_chip.at[q, i], dst_ref=from_chip.at[q, i],
                    send_sem=chip_send.at[q, i], recv_sem=chip_recv.at[q, i],
                    device_id=chip_peer, device_id_type=pl.DeviceIdType.MESH,
                )
                copy.start()
                moved["chip", q, i] = copy
            else:
                for s in range(2):
                    kept[q - 2, i, s] = both[s]

    stores = []

    def finish(q, i):
        moved[q + 2, i].wait_recv()
        moved["chip", q, i].wait_recv()
        for s in range(2):
            value = kept[q, i, s] + from_core[q + 2, i, s].astype(F32)
            out[q, i, s] = (value + from_chip[q, i, s].astype(F32)).astype(BF16)
        copy = pltpu.make_async_copy(
            out.at[q, i], out_hbm.at[pl.ds(q * 4 + i * 2, 2)], out_sem.at[q, i]
        )
        copy.start()
        stores.append(copy)

    for r, (low, size) in enumerate(quarters):
        for copy in loads[r]:
            copy.wait()
        pick(0, 1, low, low + size)
        if r == 0:
            pl.semaphore_wait(barrier, len(peers))
        p1_quarter(0, r)
    p1_expect(0)
    pick(1, 4, 0, BLOCKS)
    p1(1)
    p2(0)
    scale = measure_power()
    p3(0)
    p2(1)
    p1(2)
    p1(3)
    whiten(scale)
    p5(0)
    p3(1)
    p2(2)
    p6(0)
    p5(1)
    p2(3)
    p3(2)
    done(0)
    p6(1)
    p3(3)
    p5(2)
    cross(0)
    p5(3)
    p6(2)
    load_table.wait()
    stack(0)
    done(1)
    cross(1)
    p6(3)
    stack(1)
    done(2)
    cross(2)
    stack(2)
    done(3)
    cross(3)
    stack(3)
    for q in range(2):
        for i in range(2):
            finish(q, i)
    for copy in list(sent.values()) + list(moved.values()):
        copy.wait_send()
    for copy in stores:
        copy.wait()


def body(spectra, quality, sources):
    windows, freq_count, channels = spectra.shape[1:]
    any_space = pl.BlockSpec(memory_space=pl.ANY)
    dma = pltpu.SemaphoreType.DMA
    return pl.pallas_call(
        kernel,
        out_shape=jax.ShapeDtypeStruct((8, LAGS, channels), BF16),
        in_specs=[
            pl.BlockSpec(memory_space=pltpu.SMEM),
            any_space,
            pl.BlockSpec(memory_space=pltpu.VMEM),
            any_space,
        ],
        out_specs=any_space,
        scratch_shapes=[
            pltpu.VMEM((BLOCKS, 256, 128), BF16),
            pltpu.VMEM((LAGS, DEPTH), BF16),
            pltpu.VMEM((4, 2, ROWS, 8, 128), BF16),
            pltpu.VMEM((4, 2, 3, QUARTER, 8, 128), BF16),
            pltpu.VMEM((4, 2, QUARTER, 8, 128), BF16),
            pltpu.VMEM((4, 2, 3, PIECE, 8, 128), BF16),
            pltpu.VMEM((4, 2, PIECE, 8, 128), BF16),
            pltpu.VMEM((4, 2, 3, PIECE, 8, 128), BF16),
            pltpu.VMEM((4, 2, ROWS, 8, 128), BF16),
            pltpu.VMEM((4, DEPTH, 256), BF16),
            pltpu.VMEM((4, 2, 2, LAGS, 128), BF16),
            pltpu.VMEM((4, 2, 2, LAGS, 128), BF16),
            pltpu.VMEM((2, 2, 2, LAGS, 128), BF16),
            pltpu.VMEM((2, 2, 2, LAGS, 128), BF16),
            pltpu.VMEM((2, 2, 2, LAGS, 128), F32),
            pltpu.VMEM((2, 2, 2, LAGS, 128), BF16),
            dma((4, 32)),
            dma,
            dma((2, 2)),
            dma((4, 6, 2, 3)),
            dma((4, 6, 2, 3)),
            dma((4, 2)),
            dma((4, 2)),
            dma((2, 2)),
            dma((2, 2)),
        ],
        compiler_params=pltpu.CompilerParams(
            collective_id=0, has_side_effects=True, vmem_limit_bytes=60 * 1024 * 1024
        ),
    )(
        sources,
        spectra.reshape(2, windows, BLOCKS, 8, channels),
        quality,
        jnp.asarray(lag_table(freq_count)),
    )


def solution(mesh):
    placed = (P(None, "hour", None, "chan"), P("hour", "chan"), P())
    return jax.shard_map(
        body, mesh=mesh, in_specs=placed, out_specs=P("hour", None, "chan"), check_vma=False
    )
```

```python
import jax
import jax.numpy as jnp
import numpy as np
from jax import lax
from jax.experimental import pallas as pl
from jax.experimental.pallas import tpu as pltpu
from jax.sharding import PartitionSpec as P

LAGS = 512
F32 = jnp.float32
BF16 = jnp.bfloat16
BLOCKS = 100
ROWS = 112
QUARTER = 28
PIECE = 7
DEPTH = 1664


def lag_table(freq_count):
    bin_number = np.arange(freq_count, dtype=np.float32) + np.float32(1.0)
    lag_offset = np.arange(LAGS, dtype=np.float32) - np.float32(LAGS // 2)
    phase = np.float32(np.pi) * bin_number[:, None] * lag_offset[None, :] / np.float32(freq_count)
    table = np.concatenate([np.cos(phase), -np.sin(phase)], 0) / np.float32(freq_count)
    table = np.concatenate([table, np.zeros((DEPTH - 2 * freq_count, LAGS), np.float32)], 0)
    return np.ascontiguousarray(table.T).astype(BF16)


def kernel(
    sources, spectra, quality, table_hbm, out_hbm,
    w, table, first, got1, sum1, got2, sum2, got3, spec, part,
    to_core, from_core, to_chip, from_chip, kept, out,
    load_sem, table_sem, out_sem, send_sem, recv_sem, core_send, core_recv, chip_send, chip_recv,
):
    chan, hour = lax.axis_index("chan"), lax.axis_index("hour")
    y, zh, x = chan // 16, (chan // 4) % 4, chan % 4
    zl, core = hour // 2, hour % 2

    def at(ny, nzh, nx):
        return (ny * 16 + nzh * 4 + nx, hour)

    quarters = [(r * QUARTER, min(QUARTER, BLOCKS - r * QUARTER)) for r in range(4)]

    def along(axis, d):
        return at(y, zh, (x + d) % 4) if axis == 0 else at((y + d) % 4, zh, x)

    core_peer = (chan, zl * 2 + 1 - core)
    chip_peer = (chan, (1 - zl) * 2 + core)

    barrier = pltpu.get_barrier_semaphore()
    peers = [along(axis, d) for axis in range(2) for d in range(1, 4)]
    peers += [at(y, (zh + d) % 4, x) for d in range(1, 4)] + [core_peer, chip_peer]
    for peer in peers:
        pl.semaphore_signal(barrier, inc=1, device_id=peer, device_id_type=pl.DeviceIdType.MESH)

    loads = [
        [
            pltpu.make_async_copy(
                spectra.at[kw // 16, kw % 16, pl.ds(low, size)],
                w.at[pl.ds(low, size), pl.ds(kw * 8, 8), :], load_sem.at[r, kw],
            )
            for kw in range(32)
        ]
        for r, (low, size) in enumerate(quarters)
    ]
    for group in loads:
        for copy in group:
            copy.start()
    load_table = pltpu.make_async_copy(table_hbm, table, table_sem)
    load_table.start()

    row = lax.broadcasted_iota(jnp.int32, (32, 128), 0)
    lane = lax.broadcasted_iota(jnp.int32, (32, 128), 1)
    wanted = jnp.zeros((32, 128), jnp.int32)
    for r in range(32):
        q, i = r // 8, r % 8
        chip = (1 - zl) if q < 2 else zl
        index = (chip * 2 + i // 4) * 8 + (q % 2) * 4 + i % 4
        wanted = jnp.where(row == r, sources[index], wanted)
    onehot = jnp.where(lane + chan * 128 == wanted, 1.0, 0.0).astype(BF16)
    usable = quality[...].astype(F32)
    usable_rows = jnp.broadcast_to(usable[:, None, :], (16, 8, 128)).reshape(128, 128)
    nt = (((1,), (1,)), ((), ()))
    usable_src = lax.dot_general(
        onehot, usable_rows.astype(BF16), nt, preferred_element_type=F32
    )
    zero_tile = jnp.zeros((8, 128), BF16)
    for q in range(4):
        for k in range(2):
            for fb in range(BLOCKS, ROWS):
                first[q, k, fb] = zero_tile
    part[:, pl.ds(1600, DEPTH - 1600), :] = jnp.zeros((4, DEPTH - 1600, 256), BF16)

    def pick(q0, q1, low, high):
        hot = onehot[q0 * 8:q1 * 8]
        use = usable_src[q0 * 8:q1 * 8]

        def step(fb, _):
            got = lax.dot_general(hot, w[fb], nt, preferred_element_type=F32)
            for q in range(q0, q1):
                rows = slice((q - q0) * 8, (q - q0 + 1) * 8)
                for k in range(2):
                    value = got[rows, k * 128:(k + 1) * 128] * use[rows]
                    first[q, k, fb] = value.astype(BF16)
            return 0

        lax.fori_loop(low, high, step, 0, unroll=4)

    def send(src, dst, q, phase, k, d, peer):
        copy = pltpu.make_async_remote_copy(
            src_ref=src, dst_ref=dst,
            send_sem=send_sem.at[q, phase, k, d], recv_sem=recv_sem.at[q, phase, k, d],
            device_id=peer, device_id_type=pl.DeviceIdType.MESH,
        )
        copy.start()
        return copy

    sent = {}
    mine = [(x, y), (y, x)]

    def p1_copy(q, k, to, slot):
        peer = at(y, zh, to) if k == 0 else at(to, zh, x)
        return pltpu.make_async_remote_copy(
            src_ref=first.at[q, k, pl.ds(to * QUARTER, QUARTER)], dst_ref=got1.at[q, k, slot],
            send_sem=send_sem.at[q, 0, k, slot], recv_sem=recv_sem.at[q, 0, k, slot],
            device_id=peer, device_id_type=pl.DeviceIdType.MESH,
        )

    def p1_quarter(q, r):
        for k in range(2):
            @pl.when(mine[k][0] != r)
            def _():
                p1_copy(q, k, r, (r + 3 - mine[k][0]) % 4).start()

    def p1_expect(q):
        for k in range(2):
            for d in range(1, 4):
                sent[q, 1, k, d] = p1_copy(q, k, (mine[k][0] + d) % 4, d - 1)

    def p1(q):
        p1_expect(q)
        for k in range(2):
            for d in range(1, 4):
                sent[q, 1, k, d].start()

    def p2(q):
        for k in range(2):
            for d in range(1, 4):
                sent[q, 1, k, d].wait_recv()
            total = first[q, k, pl.ds(mine[k][0] * QUARTER, QUARTER)]
            for d in range(3):
                total = total + got1[q, k, d]
            sum1[q, k] = total
            for d in range(1, 4):
                to = (mine[k][1] + d) % 4
                sent[q, 2, k, d] = send(
                    sum1.at[q, k, pl.ds(to * PIECE, PIECE)], got2.at[q, k, d - 1],
                    q, 1, k, d - 1, along(1 - k, d),
                )

    def p3(q):
        for k in range(2):
            for d in range(1, 4):
                sent[q, 2, k, d].wait_recv()
            total = sum1[q, k, pl.ds(mine[k][1] * PIECE, PIECE)]
            for d in range(3):
                total = total + got2[q, k, d]
            sum2[q, k] = total
            for d in (2, 1, 3):
                sent[q, 3, k, d] = send(
                    sum2.at[q, k], got3.at[q, k, d - 1], q, 2, k, d - 1, at(y, (zh + d) % 4, x)
                )

    def p5(q):
        for k in range(2):
            for d in range(1, 4):
                sent[q, 3, k, d].wait_recv()
            total = sum2[q, k]
            for d in range(3):
                total = total + got3[q, k, d]
            here = spec.at[q, k, pl.ds(mine[k][0] * QUARTER + mine[k][1] * PIECE, PIECE)]
            here[...] = total
            for d in range(1, 4):
                sent[q, 5, k, d] = send(here, here, q, 4, k, d - 1, along(1 - k, d))

    def p6(q):
        for k in range(2):
            for d in range(1, 4):
                sent[q, 5, k, d].wait_recv()
            here = spec.at[q, k, pl.ds(mine[k][0] * QUARTER, QUARTER)]
            for d in range(1, 4):
                sent[q, 6, k, d] = send(here, here, q, 5, k, d - 1, along(k, d))

    def done(q):
        for k in range(2):
            for d in range(1, 4):
                sent[q, 6, k, d].wait_recv()

    def measure_power():
        def step(fb, total):
            value = w[fb].astype(F32)
            return total + value * value

        total = lax.fori_loop(0, BLOCKS, step, jnp.zeros((256, 128), F32), unroll=5)
        total = jnp.sum(total.reshape(32, 8, 128), axis=1)
        power = (total[:16] + total[16:]) / (BLOCKS * 8)
        scale = lax.rsqrt(power + 1e-06) * usable
        rows = jnp.broadcast_to(scale[:, None, :], (16, 8, 128)).reshape(128, 128)
        return jnp.concatenate([rows, rows], 0)

    def whiten(scale):
        def step(fb, _):
            w[fb] = (w[fb].astype(F32) * scale).astype(BF16)
            return 0

        lax.fori_loop(0, BLOCKS, step, 0, unroll=5)

    diagonal = (
        lax.broadcasted_iota(jnp.int32, (8, 128), 0)
        == lax.broadcasted_iota(jnp.int32, (8, 128), 1) % 8
    )
    same_window = jnp.where(
        lax.broadcasted_iota(jnp.int32, (128, 128), 0) // 8
        == lax.broadcasted_iota(jnp.int32, (128, 128), 1) // 8, 1.0, 0.0
    )

    def cross(q):
        def power_step(fb, total):
            real, imag = spec[q, 0, fb].astype(F32), spec[q, 1, fb].astype(F32)
            return total + real * real + imag * imag

        total = lax.fori_loop(0, BLOCKS, power_step, jnp.zeros((8, 128), F32), unroll=10)
        power = jnp.dot(
            total, same_window, precision=lax.Precision.HIGHEST, preferred_element_type=F32
        ) / (BLOCKS * 8)
        scale = lax.rsqrt(power + 1e-06)

        def step(pair, _):
            outs = []
            for d in range(2):
                fb = pair * 2 + d
                real = spec[q, 0, fb].astype(F32) * scale
                imag = spec[q, 1, fb].astype(F32) * scale
                upper, lower = [], []
                for s in range(8):
                    a = jnp.where(diagonal, jnp.broadcast_to(real[s:s + 1], (8, 128)), 0.0)
                    b = jnp.where(diagonal, jnp.broadcast_to(imag[s:s + 1], (8, 128)), 0.0)
                    upper.append(jnp.concatenate([a, b], 1))
                    lower.append(jnp.concatenate([-b, a], 1))
                left = jnp.concatenate(upper + lower, 0).astype(BF16)
                outs.append(jnp.dot(left, w[fb], preferred_element_type=F32).reshape(2, 8, 8, 128))
            for j in range(2):
                start = pl.multiple_of(j * 800 + pair * 16, 16)
                for s in range(8):
                    value = jnp.concatenate([outs[0][j, s], outs[1][j, s]], 0).astype(BF16)
                    part[s // 2, pl.ds(start, 16), pl.ds((s % 2) * 128, 128)] = value
            return 0

        lax.fori_loop(0, BLOCKS // 2, step, 0, unroll=5)

    def lags(pair):
        value = jnp.dot(table[...], part[pair], preferred_element_type=F32)
        return value[:, :128], value[:, 128:]

    moved = {}

    def stack(q):
        for i in range(2):
            both = lags((1 - core) * 2 + i)
            for s in range(2):
                to_core[q, i, s] = both[s].astype(BF16)
            copy = pltpu.make_async_remote_copy(
                src_ref=to_core.at[q, i], dst_ref=from_core.at[q, i],
                send_sem=core_send.at[q, i], recv_sem=core_recv.at[q, i],
                device_id=core_peer, device_id_type=pl.DeviceIdType.MESH,
            )
            copy.start()
            moved[q, i] = copy
        for i in range(2):
            both = lags(core * 2 + i)
            if q < 2:
                moved[q, i].wait_recv()
                for s in range(2):
                    to_chip[q, i, s] = (both[s] + from_core[q, i, s].astype(F32)).astype(BF16)
                copy = pltpu.make_async_remote_copy(
                    src_ref=to_chip.at[q, i], dst_ref=from_chip.at[q, i],
                    send_sem=chip_send.at[q, i], recv_sem=chip_recv.at[q, i],
                    device_id=chip_peer, device_id_type=pl.DeviceIdType.MESH,
                )
                copy.start()
                moved["chip", q, i] = copy
            else:
                for s in range(2):
                    kept[q - 2, i, s] = both[s]

    stores = []

    def finish(q, i):
        moved[q + 2, i].wait_recv()
        moved["chip", q, i].wait_recv()
        for s in range(2):
            value = kept[q, i, s] + from_core[q + 2, i, s].astype(F32)
            out[q, i, s] = (value + from_chip[q, i, s].astype(F32)).astype(BF16)
        copy = pltpu.make_async_copy(
            out.at[q, i], out_hbm.at[pl.ds(q * 4 + i * 2, 2)], out_sem.at[q, i]
        )
        copy.start()
        stores.append(copy)

    for r, (low, size) in enumerate(quarters):
        for copy in loads[r]:
            copy.wait()
        pick(0, 4, low, low + size)
        if r == 0:
            pl.semaphore_wait(barrier, len(peers))
        p1_quarter(0, r)
    p1_expect(0)
    p1(1)
    p2(0)
    p2(1)
    p1(2)
    p1(3)
    scale = measure_power()
    p3(0)
    p3(1)
    whiten(scale)
    p5(0)
    p2(2)
    p5(1)
    p2(3)
    p6(0)
    p3(2)
    p6(1)
    p3(3)
    done(0)
    cross(0)
    p5(2)
    p5(3)
    load_table.wait()
    stack(0)
    p6(2)
    p6(3)
    done(1)
    cross(1)
    stack(1)
    done(2)
    cross(2)
    stack(2)
    done(3)
    cross(3)
    stack(3)
    for q in range(2):
        for i in range(2):
            finish(q, i)
    for copy in list(sent.values()) + list(moved.values()):
        copy.wait_send()
    for copy in stores:
        copy.wait()


def body(spectra, quality, sources):
    windows, freq_count, channels = spectra.shape[1:]
    any_space = pl.BlockSpec(memory_space=pl.ANY)
    dma = pltpu.SemaphoreType.DMA
    return pl.pallas_call(
        kernel,
        out_shape=jax.ShapeDtypeStruct((8, LAGS, channels), BF16),
        in_specs=[
            pl.BlockSpec(memory_space=pltpu.SMEM),
            any_space,
            pl.BlockSpec(memory_space=pltpu.VMEM),
            any_space,
        ],
        out_specs=any_space,
        scratch_shapes=[
            pltpu.VMEM((BLOCKS, 256, 128), BF16),
            pltpu.VMEM((LAGS, DEPTH), BF16),
            pltpu.VMEM((4, 2, ROWS, 8, 128), BF16),
            pltpu.VMEM((4, 2, 3, QUARTER, 8, 128), BF16),
            pltpu.VMEM((4, 2, QUARTER, 8, 128), BF16),
            pltpu.VMEM((4, 2, 3, PIECE, 8, 128), BF16),
            pltpu.VMEM((4, 2, PIECE, 8, 128), BF16),
            pltpu.VMEM((4, 2, 3, PIECE, 8, 128), BF16),
            pltpu.VMEM((4, 2, ROWS, 8, 128), BF16),
            pltpu.VMEM((4, DEPTH, 256), BF16),
            pltpu.VMEM((4, 2, 2, LAGS, 128), BF16),
            pltpu.VMEM((4, 2, 2, LAGS, 128), BF16),
            pltpu.VMEM((2, 2, 2, LAGS, 128), BF16),
            pltpu.VMEM((2, 2, 2, LAGS, 128), BF16),
            pltpu.VMEM((2, 2, 2, LAGS, 128), F32),
            pltpu.VMEM((2, 2, 2, LAGS, 128), BF16),
            dma((4, 32)),
            dma,
            dma((2, 2)),
            dma((4, 6, 2, 3)),
            dma((4, 6, 2, 3)),
            dma((4, 2)),
            dma((4, 2)),
            dma((2, 2)),
            dma((2, 2)),
        ],
        compiler_params=pltpu.CompilerParams(
            collective_id=0, has_side_effects=True, vmem_limit_bytes=52 * 1024 * 1024
        ),
    )(
        sources,
        spectra.reshape(2, windows, BLOCKS, 8, channels),
        quality,
        jnp.asarray(lag_table(freq_count)),
    )


def solution(mesh):
    placed = (P(None, "hour", None, "chan"), P("hour", "chan"), P())
    return jax.shard_map(
        body, mesh=mesh, in_specs=placed, out_specs=P("hour", None, "chan"), check_vma=False
    )
```

```python
import jax
import jax.numpy as jnp
import numpy as np
from jax import lax
from jax.experimental import pallas as pl
from jax.experimental.pallas import tpu as pltpu
from jax.sharding import PartitionSpec as P

LAGS = 512
F32 = jnp.float32
BF16 = jnp.bfloat16
BLOCKS = 100
ROWS = 112
QUARTER = 28
PIECE = 7
DEPTH = 1664


def lag_table(freq_count):
    bin_number = np.arange(freq_count, dtype=np.float32) + np.float32(1.0)
    lag_offset = np.arange(LAGS, dtype=np.float32) - np.float32(LAGS // 2)
    phase = np.float32(np.pi) * bin_number[:, None] * lag_offset[None, :] / np.float32(freq_count)
    table = np.concatenate([np.cos(phase), -np.sin(phase)], 0) / np.float32(freq_count)
    table = np.concatenate([table, np.zeros((DEPTH - 2 * freq_count, LAGS), np.float32)], 0)
    return np.ascontiguousarray(table.T).astype(BF16)


def kernel(
    sources, spectra, quality, table_hbm, out_hbm,
    w, table, first, got1, sum1, got2, sum2, got3, spec, part,
    to_core, from_core, to_chip, from_chip, kept, out,
    load_sem, table_sem, out_sem, send_sem, recv_sem, core_send, core_recv, chip_send, chip_recv,
):
    chan, hour = lax.axis_index("chan"), lax.axis_index("hour")
    y, zh, x = chan // 16, (chan // 4) % 4, chan % 4
    zl, core = hour // 2, hour % 2

    def at(ny, nzh, nx):
        return (ny * 16 + nzh * 4 + nx, hour)

    quarters = [(r * QUARTER, min(QUARTER, BLOCKS - r * QUARTER)) for r in range(4)]

    def along(axis, d):
        return at(y, zh, (x + d) % 4) if axis == 0 else at((y + d) % 4, zh, x)

    core_peer = (chan, zl * 2 + 1 - core)
    chip_peer = (chan, (1 - zl) * 2 + core)

    barrier = pltpu.get_barrier_semaphore()
    peers = [along(axis, d) for axis in range(2) for d in range(1, 4)]
    peers += [at(y, (zh + d) % 4, x) for d in range(1, 4)] + [core_peer, chip_peer]
    for peer in peers:
        pl.semaphore_signal(barrier, inc=1, device_id=peer, device_id_type=pl.DeviceIdType.MESH)

    loads = [
        [
            pltpu.make_async_copy(
                spectra.at[kw // 16, kw % 16, pl.ds(low, size)],
                w.at[pl.ds(low, size), pl.ds(kw * 8, 8), :], load_sem.at[r, kw],
            )
            for kw in range(32)
        ]
        for r, (low, size) in enumerate(quarters)
    ]
    for group in loads:
        for copy in group:
            copy.start()
    load_table = pltpu.make_async_copy(table_hbm, table, table_sem)
    load_table.start()

    row = lax.broadcasted_iota(jnp.int32, (32, 128), 0)
    lane = lax.broadcasted_iota(jnp.int32, (32, 128), 1)
    wanted = jnp.zeros((32, 128), jnp.int32)
    for r in range(32):
        q, i = r // 8, r % 8
        chip = (1 - zl) if q < 2 else zl
        index = (chip * 2 + i // 4) * 8 + (q % 2) * 4 + i % 4
        wanted = jnp.where(row == r, sources[index], wanted)
    onehot = jnp.where(lane + chan * 128 == wanted, 1.0, 0.0).astype(BF16)
    usable = quality[...].astype(F32)
    usable_rows = jnp.broadcast_to(usable[:, None, :], (16, 8, 128)).reshape(128, 128)
    nt = (((1,), (1,)), ((), ()))
    usable_src = lax.dot_general(
        onehot, usable_rows.astype(BF16), nt, preferred_element_type=F32
    )
    zero_tile = jnp.zeros((8, 128), BF16)
    for q in range(4):
        for k in range(2):
            for fb in range(BLOCKS, ROWS):
                first[q, k, fb] = zero_tile
    part[:, pl.ds(1600, DEPTH - 1600), :] = jnp.zeros((4, DEPTH - 1600, 256), BF16)

    def pick(q0, q1, low, high):
        hot = onehot[q0 * 8:q1 * 8]
        use = usable_src[q0 * 8:q1 * 8]

        def step(fb, _):
            got = lax.dot_general(hot, w[fb], nt, preferred_element_type=F32)
            for q in range(q0, q1):
                rows = slice((q - q0) * 8, (q - q0 + 1) * 8)
                for k in range(2):
                    value = got[rows, k * 128:(k + 1) * 128] * use[rows]
                    first[q, k, fb] = value.astype(BF16)
            return 0

        lax.fori_loop(low, high, step, 0, unroll=4)

    def send(src, dst, q, phase, k, d, peer):
        copy = pltpu.make_async_remote_copy(
            src_ref=src, dst_ref=dst,
            send_sem=send_sem.at[q, phase, k, d], recv_sem=recv_sem.at[q, phase, k, d],
            device_id=peer, device_id_type=pl.DeviceIdType.MESH,
        )
        copy.start()
        return copy

    sent = {}
    mine = [(x, y), (y, x)]

    def p1_copy(q, k, to, slot):
        peer = at(y, zh, to) if k == 0 else at(to, zh, x)
        return pltpu.make_async_remote_copy(
            src_ref=first.at[q, k, pl.ds(to * QUARTER, QUARTER)], dst_ref=got1.at[q, k, slot],
            send_sem=send_sem.at[q, 0, k, slot], recv_sem=recv_sem.at[q, 0, k, slot],
            device_id=peer, device_id_type=pl.DeviceIdType.MESH,
        )

    def p1_quarter(q, r):
        for k in range(2):
            @pl.when(mine[k][0] != r)
            def _():
                p1_copy(q, k, r, (r + 3 - mine[k][0]) % 4).start()

    def p1_expect(q):
        for k in range(2):
            for d in range(1, 4):
                sent[q, 1, k, d] = p1_copy(q, k, (mine[k][0] + d) % 4, d - 1)

    def p1(q):
        p1_expect(q)
        for k in range(2):
            for d in range(1, 4):
                sent[q, 1, k, d].start()

    def p2(q):
        for k in range(2):
            for d in range(1, 4):
                sent[q, 1, k, d].wait_recv()
            total = first[q, k, pl.ds(mine[k][0] * QUARTER, QUARTER)]
            for d in range(3):
                total = total + got1[q, k, d]
            sum1[q, k] = total
            for d in range(1, 4):
                to = (mine[k][1] + d) % 4
                sent[q, 2, k, d] = send(
                    sum1.at[q, k, pl.ds(to * PIECE, PIECE)], got2.at[q, k, d - 1],
                    q, 1, k, d - 1, along(1 - k, d),
                )

    def p3(q):
        for k in range(2):
            for d in range(1, 4):
                sent[q, 2, k, d].wait_recv()
            total = sum1[q, k, pl.ds(mine[k][1] * PIECE, PIECE)]
            for d in range(3):
                total = total + got2[q, k, d]
            sum2[q, k] = total
            for d in (2, 1, 3):
                sent[q, 3, k, d] = send(
                    sum2.at[q, k], got3.at[q, k, d - 1], q, 2, k, d - 1, at(y, (zh + d) % 4, x)
                )

    def p5(q):
        for k in range(2):
            for d in range(1, 4):
                sent[q, 3, k, d].wait_recv()
            total = sum2[q, k]
            for d in range(3):
                total = total + got3[q, k, d]
            here = spec.at[q, k, pl.ds(mine[k][0] * QUARTER + mine[k][1] * PIECE, PIECE)]
            here[...] = total
            for d in range(1, 4):
                sent[q, 5, k, d] = send(here, here, q, 4, k, d - 1, along(1 - k, d))

    def p6(q):
        for k in range(2):
            for d in range(1, 4):
                sent[q, 5, k, d].wait_recv()
            here = spec.at[q, k, pl.ds(mine[k][0] * QUARTER, QUARTER)]
            for d in range(1, 4):
                sent[q, 6, k, d] = send(here, here, q, 5, k, d - 1, along(k, d))

    def done(q):
        for k in range(2):
            for d in range(1, 4):
                sent[q, 6, k, d].wait_recv()

    def measure_power():
        def step(fb, total):
            value = w[fb].astype(F32)
            return total + value * value

        total = lax.fori_loop(0, BLOCKS, step, jnp.zeros((256, 128), F32), unroll=5)
        total = jnp.sum(total.reshape(32, 8, 128), axis=1)
        power = (total[:16] + total[16:]) / (BLOCKS * 8)
        scale = lax.rsqrt(power + 1e-06) * usable
        rows = jnp.broadcast_to(scale[:, None, :], (16, 8, 128)).reshape(128, 128)
        return jnp.concatenate([rows, rows], 0)

    def whiten(scale):
        def step(fb, _):
            w[fb] = (w[fb].astype(F32) * scale).astype(BF16)
            return 0

        lax.fori_loop(0, BLOCKS, step, 0, unroll=5)

    diagonal = (
        lax.broadcasted_iota(jnp.int32, (8, 128), 0)
        == lax.broadcasted_iota(jnp.int32, (8, 128), 1) % 8
    )
    same_window = jnp.where(
        lax.broadcasted_iota(jnp.int32, (128, 128), 0) // 8
        == lax.broadcasted_iota(jnp.int32, (128, 128), 1) // 8, 1.0, 0.0
    )

    def cross(q):
        def power_step(fb, total):
            real, imag = spec[q, 0, fb].astype(F32), spec[q, 1, fb].astype(F32)
            return total + real * real + imag * imag

        total = lax.fori_loop(0, BLOCKS, power_step, jnp.zeros((8, 128), F32), unroll=10)
        power = jnp.dot(
            total, same_window, precision=lax.Precision.HIGHEST, preferred_element_type=F32
        ) / (BLOCKS * 8)
        scale = lax.rsqrt(power + 1e-06)

        def step(pair, _):
            outs = []
            for d in range(2):
                fb = pair * 2 + d
                real = spec[q, 0, fb].astype(F32) * scale
                imag = spec[q, 1, fb].astype(F32) * scale
                upper, lower = [], []
                for s in range(8):
                    a = jnp.where(diagonal, jnp.broadcast_to(real[s:s + 1], (8, 128)), 0.0)
                    b = jnp.where(diagonal, jnp.broadcast_to(imag[s:s + 1], (8, 128)), 0.0)
                    upper.append(jnp.concatenate([a, b], 1))
                    lower.append(jnp.concatenate([-b, a], 1))
                left = jnp.concatenate(upper + lower, 0).astype(BF16)
                outs.append(jnp.dot(left, w[fb], preferred_element_type=F32).reshape(2, 8, 8, 128))
            for j in range(2):
                start = pl.multiple_of(j * 800 + pair * 16, 16)
                for s in range(8):
                    value = jnp.concatenate([outs[0][j, s], outs[1][j, s]], 0).astype(BF16)
                    part[s // 2, pl.ds(start, 16), pl.ds((s % 2) * 128, 128)] = value
            return 0

        lax.fori_loop(0, BLOCKS // 2, step, 0, unroll=10)

    def lags(pair):
        value = jnp.dot(table[...], part[pair], preferred_element_type=F32)
        return value[:, :128], value[:, 128:]

    moved = {}

    def stack(q):
        for i in range(2):
            both = lags((1 - core) * 2 + i)
            for s in range(2):
                to_core[q, i, s] = both[s].astype(BF16)
            copy = pltpu.make_async_remote_copy(
                src_ref=to_core.at[q, i], dst_ref=from_core.at[q, i],
                send_sem=core_send.at[q, i], recv_sem=core_recv.at[q, i],
                device_id=core_peer, device_id_type=pl.DeviceIdType.MESH,
            )
            copy.start()
            moved[q, i] = copy
        for i in range(2):
            both = lags(core * 2 + i)
            if q < 2:
                moved[q, i].wait_recv()
                for s in range(2):
                    to_chip[q, i, s] = (both[s] + from_core[q, i, s].astype(F32)).astype(BF16)
                copy = pltpu.make_async_remote_copy(
                    src_ref=to_chip.at[q, i], dst_ref=from_chip.at[q, i],
                    send_sem=chip_send.at[q, i], recv_sem=chip_recv.at[q, i],
                    device_id=chip_peer, device_id_type=pl.DeviceIdType.MESH,
                )
                copy.start()
                moved["chip", q, i] = copy
            else:
                for s in range(2):
                    kept[q - 2, i, s] = both[s]

    stores = []

    def finish(q, i):
        moved[q + 2, i].wait_recv()
        moved["chip", q, i].wait_recv()
        for s in range(2):
            value = kept[q, i, s] + from_core[q + 2, i, s].astype(F32)
            out[q, i, s] = (value + from_chip[q, i, s].astype(F32)).astype(BF16)
        copy = pltpu.make_async_copy(
            out.at[q, i], out_hbm.at[pl.ds(q * 4 + i * 2, 2)], out_sem.at[q, i]
        )
        copy.start()
        stores.append(copy)

    for r, (low, size) in enumerate(quarters):
        for copy in loads[r]:
            copy.wait()
        pick(0, 4, low, low + size)
        if r == 0:
            pl.semaphore_wait(barrier, len(peers))
        p1_quarter(0, r)
    p1_expect(0)
    p1(1)
    p2(0)
    p2(1)
    p1(2)
    p1(3)
    scale = measure_power()
    p3(0)
    p3(1)
    whiten(scale)
    p5(0)
    p2(2)
    p5(1)
    p2(3)
    p6(0)
    p3(2)
    p6(1)
    p3(3)
    done(0)
    cross(0)
    p5(2)
    p5(3)
    load_table.wait()
    stack(0)
    p6(2)
    p6(3)
    done(1)
    cross(1)
    stack(1)
    done(2)
    cross(2)
    stack(2)
    done(3)
    cross(3)
    stack(3)
    for q in range(2):
        for i in range(2):
            finish(q, i)
    for copy in list(sent.values()) + list(moved.values()):
        copy.wait_send()
    for copy in stores:
        copy.wait()


def body(spectra, quality, sources):
    windows, freq_count, channels = spectra.shape[1:]
    any_space = pl.BlockSpec(memory_space=pl.ANY)
    dma = pltpu.SemaphoreType.DMA
    return pl.pallas_call(
        kernel,
        out_shape=jax.ShapeDtypeStruct((8, LAGS, channels), BF16),
        in_specs=[
            pl.BlockSpec(memory_space=pltpu.SMEM),
            any_space,
            pl.BlockSpec(memory_space=pltpu.VMEM),
            any_space,
        ],
        out_specs=any_space,
        scratch_shapes=[
            pltpu.VMEM((BLOCKS, 256, 128), BF16),
            pltpu.VMEM((LAGS, DEPTH), BF16),
            pltpu.VMEM((4, 2, ROWS, 8, 128), BF16),
            pltpu.VMEM((4, 2, 3, QUARTER, 8, 128), BF16),
            pltpu.VMEM((4, 2, QUARTER, 8, 128), BF16),
            pltpu.VMEM((4, 2, 3, PIECE, 8, 128), BF16),
            pltpu.VMEM((4, 2, PIECE, 8, 128), BF16),
            pltpu.VMEM((4, 2, 3, PIECE, 8, 128), BF16),
            pltpu.VMEM((4, 2, ROWS, 8, 128), BF16),
            pltpu.VMEM((4, DEPTH, 256), BF16),
            pltpu.VMEM((4, 2, 2, LAGS, 128), BF16),
            pltpu.VMEM((4, 2, 2, LAGS, 128), BF16),
            pltpu.VMEM((2, 2, 2, LAGS, 128), BF16),
            pltpu.VMEM((2, 2, 2, LAGS, 128), BF16),
            pltpu.VMEM((2, 2, 2, LAGS, 128), F32),
            pltpu.VMEM((2, 2, 2, LAGS, 128), BF16),
            dma((4, 32)),
            dma,
            dma((2, 2)),
            dma((4, 6, 2, 3)),
            dma((4, 6, 2, 3)),
            dma((4, 2)),
            dma((4, 2)),
            dma((2, 2)),
            dma((2, 2)),
        ],
        compiler_params=pltpu.CompilerParams(
            collective_id=0, has_side_effects=True, vmem_limit_bytes=52 * 1024 * 1024
        ),
    )(
        sources,
        spectra.reshape(2, windows, BLOCKS, 8, channels),
        quality,
        jnp.asarray(lag_table(freq_count)),
    )


def solution(mesh):
    placed = (P(None, "hour", None, "chan"), P("hour", "chan"), P())
    return jax.shard_map(
        body, mesh=mesh, in_specs=placed, out_specs=P("hour", None, "chan"), check_vma=False
    )
```

```python
import jax
import jax.numpy as jnp
import numpy as np
from jax import lax
from jax.experimental import pallas as pl
from jax.experimental.pallas import tpu as pltpu
from jax.sharding import PartitionSpec as P

LAGS = 512
F32 = jnp.float32
BF16 = jnp.bfloat16
BLOCKS = 100
ROWS = 112
QUARTER = 28
PIECE = 7
DEPTH = 1664


def lag_table(freq_count):
    bin_number = np.arange(freq_count, dtype=np.float32) + np.float32(1.0)
    lag_offset = np.arange(LAGS, dtype=np.float32) - np.float32(LAGS // 2)
    phase = np.float32(np.pi) * bin_number[:, None] * lag_offset[None, :] / np.float32(freq_count)
    table = np.concatenate([np.cos(phase), -np.sin(phase)], 0) / np.float32(freq_count)
    table = np.concatenate([table, np.zeros((DEPTH - 2 * freq_count, LAGS), np.float32)], 0)
    return np.ascontiguousarray(table.T).astype(BF16)


def kernel(
    sources, spectra, quality, table_hbm, out_hbm,
    w, table, first, got1, sum1, got2, sum2, got3, spec, part,
    to_core, from_core, to_chip, from_chip, kept, out,
    load_sem, table_sem, out_sem, send_sem, recv_sem, core_send, core_recv, chip_send, chip_recv,
):
    chan, hour = lax.axis_index("chan"), lax.axis_index("hour")
    y, zh, x = chan // 16, (chan // 4) % 4, chan % 4
    zl, core = hour // 2, hour % 2

    def at(ny, nzh, nx):
        return (ny * 16 + nzh * 4 + nx, hour)

    quarters = [(r * QUARTER, min(QUARTER, BLOCKS - r * QUARTER)) for r in range(4)]

    def along(axis, d):
        return at(y, zh, (x + d) % 4) if axis == 0 else at((y + d) % 4, zh, x)

    core_peer = (chan, zl * 2 + 1 - core)
    chip_peer = (chan, (1 - zl) * 2 + core)

    barrier = pltpu.get_barrier_semaphore()
    peers = [along(axis, d) for axis in range(2) for d in range(1, 4)]
    peers += [at(y, (zh + d) % 4, x) for d in range(1, 4)] + [core_peer, chip_peer]
    for peer in peers:
        pl.semaphore_signal(barrier, inc=1, device_id=peer, device_id_type=pl.DeviceIdType.MESH)

    loads = [
        [
            pltpu.make_async_copy(
                spectra.at[kw // 16, kw % 16, pl.ds(low, size)],
                w.at[pl.ds(low, size), pl.ds(kw * 8, 8), :], load_sem.at[r, kw],
            )
            for kw in range(32)
        ]
        for r, (low, size) in enumerate(quarters)
    ]
    for group in loads:
        for copy in group:
            copy.start()
    load_table = pltpu.make_async_copy(table_hbm, table, table_sem)
    load_table.start()

    row = lax.broadcasted_iota(jnp.int32, (32, 128), 0)
    lane = lax.broadcasted_iota(jnp.int32, (32, 128), 1)
    wanted = jnp.zeros((32, 128), jnp.int32)
    for r in range(32):
        q, i = r // 8, r % 8
        chip = (1 - zl) if q < 2 else zl
        index = (chip * 2 + i // 4) * 8 + (q % 2) * 4 + i % 4
        wanted = jnp.where(row == r, sources[index], wanted)
    onehot = jnp.where(lane + chan * 128 == wanted, 1.0, 0.0).astype(BF16)
    usable = quality[...].astype(F32)
    usable_rows = jnp.broadcast_to(usable[:, None, :], (16, 8, 128)).reshape(128, 128)
    nt = (((1,), (1,)), ((), ()))
    usable_src = lax.dot_general(
        onehot, usable_rows.astype(BF16), nt, preferred_element_type=F32
    )
    zero_tile = jnp.zeros((8, 128), BF16)
    for q in range(4):
        for k in range(2):
            for fb in range(BLOCKS, ROWS):
                first[q, k, fb] = zero_tile
    part[:, pl.ds(1600, DEPTH - 1600), :] = jnp.zeros((4, DEPTH - 1600, 256), BF16)

    def pick(q0, q1, low, high):
        hot = onehot[q0 * 8:q1 * 8]
        use = usable_src[q0 * 8:q1 * 8]

        def step(fb, _):
            got = lax.dot_general(hot, w[fb], nt, preferred_element_type=F32)
            for q in range(q0, q1):
                rows = slice((q - q0) * 8, (q - q0 + 1) * 8)
                for k in range(2):
                    value = got[rows, k * 128:(k + 1) * 128] * use[rows]
                    first[q, k, fb] = value.astype(BF16)
            return 0

        lax.fori_loop(low, high, step, 0, unroll=4)

    def send(src, dst, q, phase, k, d, peer):
        copy = pltpu.make_async_remote_copy(
            src_ref=src, dst_ref=dst,
            send_sem=send_sem.at[q, phase, k, d], recv_sem=recv_sem.at[q, phase, k, d],
            device_id=peer, device_id_type=pl.DeviceIdType.MESH,
        )
        copy.start()
        return copy

    sent = {}
    mine = [(x, y), (y, x)]

    def p1_copy(q, k, to, slot):
        peer = at(y, zh, to) if k == 0 else at(to, zh, x)
        return pltpu.make_async_remote_copy(
            src_ref=first.at[q, k, pl.ds(to * QUARTER, QUARTER)], dst_ref=got1.at[q, k, slot],
            send_sem=send_sem.at[q, 0, k, slot], recv_sem=recv_sem.at[q, 0, k, slot],
            device_id=peer, device_id_type=pl.DeviceIdType.MESH,
        )

    def p1_quarter(q, r):
        for k in range(2):
            @pl.when(mine[k][0] != r)
            def _():
                p1_copy(q, k, r, (r + 3 - mine[k][0]) % 4).start()

    def p1_expect(q):
        for k in range(2):
            for d in range(1, 4):
                sent[q, 1, k, d] = p1_copy(q, k, (mine[k][0] + d) % 4, d - 1)

    def p1(q):
        p1_expect(q)
        for k in range(2):
            for d in range(1, 4):
                sent[q, 1, k, d].start()

    def p2(q):
        for k in range(2):
            for d in range(1, 4):
                sent[q, 1, k, d].wait_recv()
            total = first[q, k, pl.ds(mine[k][0] * QUARTER, QUARTER)]
            for d in range(3):
                total = total + got1[q, k, d]
            sum1[q, k] = total
            for d in range(1, 4):
                to = (mine[k][1] + d) % 4
                sent[q, 2, k, d] = send(
                    sum1.at[q, k, pl.ds(to * PIECE, PIECE)], got2.at[q, k, d - 1],
                    q, 1, k, d - 1, along(1 - k, d),
                )

    def p3(q):
        for k in range(2):
            for d in range(1, 4):
                sent[q, 2, k, d].wait_recv()
            total = sum1[q, k, pl.ds(mine[k][1] * PIECE, PIECE)]
            for d in range(3):
                total = total + got2[q, k, d]
            sum2[q, k] = total
            for d in (2, 1, 3):
                sent[q, 3, k, d] = send(
                    sum2.at[q, k], got3.at[q, k, d - 1], q, 2, k, d - 1, at(y, (zh + d) % 4, x)
                )

    def p5(q):
        for k in range(2):
            for d in range(1, 4):
                sent[q, 3, k, d].wait_recv()
            total = sum2[q, k]
            for d in range(3):
                total = total + got3[q, k, d]
            here = spec.at[q, k, pl.ds(mine[k][0] * QUARTER + mine[k][1] * PIECE, PIECE)]
            here[...] = total
            for d in range(1, 4):
                sent[q, 5, k, d] = send(here, here, q, 4, k, d - 1, along(1 - k, d))

    def p6(q):
        for k in range(2):
            for d in range(1, 4):
                sent[q, 5, k, d].wait_recv()
            here = spec.at[q, k, pl.ds(mine[k][0] * QUARTER, QUARTER)]
            for d in range(1, 4):
                sent[q, 6, k, d] = send(here, here, q, 5, k, d - 1, along(k, d))

    def done(q):
        for k in range(2):
            for d in range(1, 4):
                sent[q, 6, k, d].wait_recv()

    def measure_power():
        def step(fb, total):
            value = w[fb].astype(F32)
            return total + value * value

        total = lax.fori_loop(0, BLOCKS, step, jnp.zeros((256, 128), F32), unroll=5)
        total = jnp.sum(total.reshape(32, 8, 128), axis=1)
        power = (total[:16] + total[16:]) / (BLOCKS * 8)
        scale = lax.rsqrt(power + 1e-06) * usable
        rows = jnp.broadcast_to(scale[:, None, :], (16, 8, 128)).reshape(128, 128)
        return jnp.concatenate([rows, rows], 0)

    def whiten(scale):
        def step(fb, _):
            w[fb] = (w[fb].astype(F32) * scale).astype(BF16)
            return 0

        lax.fori_loop(0, BLOCKS, step, 0, unroll=5)

    diagonal = (
        lax.broadcasted_iota(jnp.int32, (8, 128), 0)
        == lax.broadcasted_iota(jnp.int32, (8, 128), 1) % 8
    )
    same_window = jnp.where(
        lax.broadcasted_iota(jnp.int32, (128, 128), 0) // 8
        == lax.broadcasted_iota(jnp.int32, (128, 128), 1) // 8, 1.0, 0.0
    )

    def cross(q):
        def power_step(fb, total):
            real, imag = spec[q, 0, fb].astype(F32), spec[q, 1, fb].astype(F32)
            return total + real * real + imag * imag

        total = lax.fori_loop(0, BLOCKS, power_step, jnp.zeros((8, 128), F32), unroll=10)
        power = jnp.dot(
            total, same_window, precision=lax.Precision.HIGHEST, preferred_element_type=F32
        ) / (BLOCKS * 8)
        scale = lax.rsqrt(power + 1e-06)

        def step(pair, _):
            outs = []
            for d in range(2):
                fb = pair * 2 + d
                real = spec[q, 0, fb].astype(F32) * scale
                imag = spec[q, 1, fb].astype(F32) * scale
                upper, lower = [], []
                for s in range(8):
                    a = jnp.where(diagonal, jnp.broadcast_to(real[s:s + 1], (8, 128)), 0.0)
                    b = jnp.where(diagonal, jnp.broadcast_to(imag[s:s + 1], (8, 128)), 0.0)
                    upper.append(jnp.concatenate([a, b], 1))
                    lower.append(jnp.concatenate([-b, a], 1))
                left = jnp.concatenate(upper + lower, 0).astype(BF16)
                outs.append(jnp.dot(left, w[fb], preferred_element_type=F32).reshape(2, 8, 8, 128))
            for j in range(2):
                start = pl.multiple_of(j * 800 + pair * 16, 16)
                for s in range(8):
                    value = jnp.concatenate([outs[0][j, s], outs[1][j, s]], 0).astype(BF16)
                    part[s // 2, pl.ds(start, 16), pl.ds((s % 2) * 128, 128)] = value
            return 0

        lax.fori_loop(0, BLOCKS // 2, step, 0, unroll=25)

    def lags(pair):
        value = jnp.dot(table[...], part[pair], preferred_element_type=F32)
        return value[:, :128], value[:, 128:]

    moved = {}

    def stack(q):
        for i in range(2):
            both = lags((1 - core) * 2 + i)
            for s in range(2):
                to_core[q, i, s] = both[s].astype(BF16)
            copy = pltpu.make_async_remote_copy(
                src_ref=to_core.at[q, i], dst_ref=from_core.at[q, i],
                send_sem=core_send.at[q, i], recv_sem=core_recv.at[q, i],
                device_id=core_peer, device_id_type=pl.DeviceIdType.MESH,
            )
            copy.start()
            moved[q, i] = copy
        for i in range(2):
            both = lags(core * 2 + i)
            if q < 2:
                moved[q, i].wait_recv()
                for s in range(2):
                    to_chip[q, i, s] = (both[s] + from_core[q, i, s].astype(F32)).astype(BF16)
                copy = pltpu.make_async_remote_copy(
                    src_ref=to_chip.at[q, i], dst_ref=from_chip.at[q, i],
                    send_sem=chip_send.at[q, i], recv_sem=chip_recv.at[q, i],
                    device_id=chip_peer, device_id_type=pl.DeviceIdType.MESH,
                )
                copy.start()
                moved["chip", q, i] = copy
            else:
                for s in range(2):
                    kept[q - 2, i, s] = both[s]

    stores = []

    def finish(q, i):
        moved[q + 2, i].wait_recv()
        moved["chip", q, i].wait_recv()
        for s in range(2):
            value = kept[q, i, s] + from_core[q + 2, i, s].astype(F32)
            out[q, i, s] = (value + from_chip[q, i, s].astype(F32)).astype(BF16)
        copy = pltpu.make_async_copy(
            out.at[q, i], out_hbm.at[pl.ds(q * 4 + i * 2, 2)], out_sem.at[q, i]
        )
        copy.start()
        stores.append(copy)

    for r, (low, size) in enumerate(quarters):
        for copy in loads[r]:
            copy.wait()
        pick(0, 4, low, low + size)
        if r == 0:
            pl.semaphore_wait(barrier, len(peers))
        p1_quarter(0, r)
    p1_expect(0)
    p1(1)
    p2(0)
    p2(1)
    p1(2)
    p1(3)
    scale = measure_power()
    p3(0)
    p3(1)
    whiten(scale)
    p5(0)
    p2(2)
    p5(1)
    p2(3)
    p6(0)
    p3(2)
    p6(1)
    p3(3)
    done(0)
    cross(0)
    p5(2)
    p5(3)
    load_table.wait()
    stack(0)
    p6(2)
    p6(3)
    done(1)
    cross(1)
    stack(1)
    done(2)
    cross(2)
    stack(2)
    done(3)
    cross(3)
    stack(3)
    for q in range(2):
        for i in range(2):
            finish(q, i)
    for copy in list(sent.values()) + list(moved.values()):
        copy.wait_send()
    for copy in stores:
        copy.wait()


def body(spectra, quality, sources):
    windows, freq_count, channels = spectra.shape[1:]
    any_space = pl.BlockSpec(memory_space=pl.ANY)
    dma = pltpu.SemaphoreType.DMA
    return pl.pallas_call(
        kernel,
        out_shape=jax.ShapeDtypeStruct((8, LAGS, channels), BF16),
        in_specs=[
            pl.BlockSpec(memory_space=pltpu.SMEM),
            any_space,
            pl.BlockSpec(memory_space=pltpu.VMEM),
            any_space,
        ],
        out_specs=any_space,
        scratch_shapes=[
            pltpu.VMEM((BLOCKS, 256, 128), BF16),
            pltpu.VMEM((LAGS, DEPTH), BF16),
            pltpu.VMEM((4, 2, ROWS, 8, 128), BF16),
            pltpu.VMEM((4, 2, 3, QUARTER, 8, 128), BF16),
            pltpu.VMEM((4, 2, QUARTER, 8, 128), BF16),
            pltpu.VMEM((4, 2, 3, PIECE, 8, 128), BF16),
            pltpu.VMEM((4, 2, PIECE, 8, 128), BF16),
            pltpu.VMEM((4, 2, 3, PIECE, 8, 128), BF16),
            pltpu.VMEM((4, 2, ROWS, 8, 128), BF16),
            pltpu.VMEM((4, DEPTH, 256), BF16),
            pltpu.VMEM((4, 2, 2, LAGS, 128), BF16),
            pltpu.VMEM((4, 2, 2, LAGS, 128), BF16),
            pltpu.VMEM((2, 2, 2, LAGS, 128), BF16),
            pltpu.VMEM((2, 2, 2, LAGS, 128), BF16),
            pltpu.VMEM((2, 2, 2, LAGS, 128), F32),
            pltpu.VMEM((2, 2, 2, LAGS, 128), BF16),
            dma((4, 32)),
            dma,
            dma((2, 2)),
            dma((4, 6, 2, 3)),
            dma((4, 6, 2, 3)),
            dma((4, 2)),
            dma((4, 2)),
            dma((2, 2)),
            dma((2, 2)),
        ],
        compiler_params=pltpu.CompilerParams(
            collective_id=0, has_side_effects=True, vmem_limit_bytes=52 * 1024 * 1024
        ),
    )(
        sources,
        spectra.reshape(2, windows, BLOCKS, 8, channels),
        quality,
        jnp.asarray(lag_table(freq_count)),
    )


def solution(mesh):
    placed = (P(None, "hour", None, "chan"), P("hour", "chan"), P())
    return jax.shard_map(
        body, mesh=mesh, in_specs=placed, out_specs=P("hour", None, "chan"), check_vma=False
    )
```
